32 devices in a mesh: rows: 2 (over x), cent: 16 (over z, y, core).
Axes of the slice: x: 2, y: 2, z: 4, core: 2. Of those that a mesh axis runs over, the one named last changes fastest.
Arguments:
- embeddings: bfloat16 [2048, 768], P(('rows', 'cent')), may hold values from -33 to 33
- centroids: bfloat16 [2048, 768], P('cent'), may hold values from -4 to 4
- group_length: int32 [2], P('rows'), may hold values from 256 to 1024, as said below
Outputs:
- new_centroids: bfloat16 [2048, 768], P('cent')
- new_moments: bfloat16 [2048, 768], P('cent')
- loglik: float32 [2048], P(('rows', 'cent'))
The draws below stay inside these ranges and needn't reach their ends.
Inputs may be any that keep to these rules, and one draw needn't show every extreme that they name: Row group g uses its first group_length[g] of its 1024 row slots; at least one group uses all of them.
All inputs are finite; a program needn't handle non-finite values.
Results may differ from the reference program's by a relative error of at most 0.0047.
Values may be sent and summed in bfloat16 or wider, within the bound.
A program may use at most 64 MiB of HBM per device.

```python
import math
import jax
import jax.numpy as jnp
from jax import lax

D = 768
K = 2048
ROWS_GROUP = 1024
GROUPS = 2
ROWS = 2048


def centroid_table(key):
    values_base = jax.random.normal(jax.random.fold_in(key, 71), (K, D), jnp.float32)
    values_base = jnp.clip(values_base, -4.0, 4.0)
    row_index = jnp.arange(K, dtype=jnp.int32)
    partner = row_index % 61 == 1
    shifted = jnp.roll(jnp.roll(values_base, 1, axis=1), 1, axis=0)
    return jnp.where(partner[:, None], shifted, values_base)


def draw_centroids(key, part):
    return centroid_table(key).astype(jnp.bfloat16)


def draw_embeddings(key, part):
    values_base = jnp.clip(jax.random.normal(jax.random.fold_in(key, 72), (ROWS, D), jnp.float32), -6.0, 6.0)
    return values_base.astype(jnp.bfloat16)


def draw_group_length(key, part):
    lengths = jax.random.randint(jax.random.fold_in(key, 81), (GROUPS,), ROWS_GROUP // 4, ROWS_GROUP + 1, dtype=jnp.int32)
    full_group = jax.random.randint(jax.random.fold_in(key, 82), (), 0, GROUPS, dtype=jnp.int32)
    return jnp.where(jnp.arange(GROUPS, dtype=jnp.int32) == full_group, ROWS_GROUP, lengths).astype(jnp.int32)


def setup_inputs(seed: int = 0) -> dict:
    splits = jax.random.split(jax.random.key(seed), 4)
    embeddings = draw_embeddings(jax.random.fold_in(splits[3], 71), 0)
    centroids = draw_centroids(jax.random.fold_in(splits[3], 71), 0)
    group_length = draw_group_length(jax.random.fold_in(splits[3], 71), 0)
    return dict(embeddings=embeddings, centroids=centroids, group_length=group_length)


def reference(embeddings, centroids, group_length):
    cent_wide = centroids.astype(jnp.float32)
    squared_norm = lax.optimization_barrier(jnp.sum(cent_wide * cent_wide, axis=1))
    factor = 3.0 / math.sqrt(D)
    row_blocks = embeddings.reshape(GROUPS, ROWS_GROUP, D)

    def group_step(state_in, group_item):
        weighted, moments, weight_mass = state_in
        block_rows, used_rows = group_item
        inner = jnp.dot(block_rows, centroids.T, preferred_element_type=jnp.float32)
        logits = factor * (inner - 0.5 * squared_norm[None, :])
        row_lse = jax.nn.logsumexp(logits, axis=1)
        valid_rows = jnp.arange(ROWS_GROUP, dtype=jnp.int32) < used_rows
        responsibility = jnp.where(valid_rows[:, None], jnp.exp(logits - row_lse[:, None]), 0.0).astype(jnp.bfloat16)
        rows_wide = block_rows.astype(jnp.float32)
        squares = (rows_wide * rows_wide).astype(jnp.bfloat16)
        weighted = weighted + jnp.dot(responsibility.T, block_rows, preferred_element_type=jnp.float32)
        moments = moments + jnp.dot(responsibility.T, squares, preferred_element_type=jnp.float32)
        weight_mass = weight_mass + lax.optimization_barrier(jnp.sum(responsibility.astype(jnp.float32), axis=0))
        loglik = jnp.where(valid_rows, row_lse, jnp.zeros_like(row_lse))
        return ((weighted, moments, weight_mass), loglik)
    zero_state = (jnp.zeros((K, D), jnp.float32), jnp.zeros((K, D), jnp.float32), jnp.zeros((K,), jnp.float32))
    totals, loglik = lax.scan(group_step, zero_state, (row_blocks, group_length))
    weighted, moments, weight_mass = totals
    denominator = weight_mass[:, None] + 1.0
    new_centroids = ((weighted + 1.0 * cent_wide) / denominator).astype(jnp.bfloat16)
    new_moments = ((moments + 1.0) / denominator).astype(jnp.bfloat16)
    return (new_centroids, new_moments, loglik.reshape(ROWS))
```

```python
import functools
import math

import jax
import jax.numpy as jnp
from jax import lax
from jax.experimental import pallas as pl
from jax.experimental.pallas import tpu as pltpu
from jax.sharding import PartitionSpec as P

score_factor = 3.0
prior_weight = 1.0
MESH = pl.DeviceIdType.MESH
contract_width = (((1,), (1,)), ((), ()))
contract_rows = (((1,), (0,)), ((), ()))


def kernel(
    groups, shards, column_step,
    length_ref, emb_ref, cent_ref,
    cent_out, mom_out, lik_out,
    rows_all, squares, weights, parts, stats, masses,
    own_sem, z_send, z_recv, y_send, y_recv, c_send, c_recv,
    p_send, p_recv, s_send, s_recv, m_send, m_recv,
):
    g = lax.axis_index("rows")
    i = lax.axis_index("cent")
    row_count, width = emb_ref.shape
    cents = cent_ref.shape[0]
    total = shards * row_count
    line = shards // 4
    spot = lax.rem(i, 4)
    place = i // 4
    core = lax.rem(i, 2)
    core_peer = i + 1 - 2 * core
    y_peer = place * 4 + lax.rem(spot + 2, 4)
    factor = score_factor / math.sqrt(width)

    def along(step):
        return lax.rem(place + step, line) * 4 + spot

    def behind(step, where):
        return lax.rem(place + line - step, line) * 4 + where

    def across(step):
        return lax.rem(g + step, groups)

    barrier = pltpu.get_barrier_semaphore()
    peers = [(g, along(s)) for s in range(1, line)]
    peers += [(g, y_peer), (g, core_peer)]
    peers += [(across(s), i) for s in range(1, groups)]
    for peer in peers:
        pl.semaphore_signal(barrier, inc=1, device_id=peer, device_id_type=MESH)
    own = pltpu.make_async_copy(emb_ref, rows_all.at[i], own_sem)
    own.start()
    cent_wide = cent_ref[...].astype(jnp.float32)
    half_norm = 0.5 * jnp.sum(cent_wide * cent_wide, axis=1, keepdims=True)
    pl.semaphore_wait(barrier, len(peers))

    def send(src, dst, send_sem, recv_sem, peer):
        copy = pltpu.make_async_remote_copy(
            src_ref=src, dst_ref=dst, send_sem=send_sem, recv_sem=recv_sem,
            device_id=peer, device_id_type=MESH,
        )
        copy.start()
        return copy

    sent = []
    z_copies = {}
    y_copies = {}
    c_copies = {}
    mine = rows_all.at[i]
    y_copies[0] = send(emb_ref, mine, y_send.at[0], y_recv.at[0], (g, y_peer))
    for s in range(1, line):
        z_copies[s] = send(emb_ref, mine, z_send.at[s], z_recv.at[s], (g, along(s)))
    c_copies[0] = send(emb_ref, mine, c_send.at[0], c_recv.at[0], (g, core_peer))
    for s in range(1, line):
        z_copies[s].wait_recv()
        slot = rows_all.at[behind(s, spot)]
        y_copies[s] = send(slot, slot, y_send.at[s], y_recv.at[s], (g, y_peer))
        c_copies[s] = send(slot, slot, c_send.at[s], c_recv.at[s], (g, core_peer))
    for s in range(line):
        y_copies[s].wait_recv()
        slot = rows_all.at[behind(s, lax.rem(spot + 2, 4))]
        k = line + s
        c_copies[k] = send(slot, slot, c_send.at[k], c_recv.at[k], (g, core_peer))
    for k in range(2 * line):
        c_copies[k].wait_recv()
    own.wait()
    for copies in (z_copies, y_copies, c_copies):
        sent += list(copies.values())

    slots = max(1, min(shards, 512 // row_count))
    chunk = slots * row_count

    def score(k, carry):
        first = k * slots
        columns = k * chunk
        if not isinstance(k, int):
            columns = pl.multiple_of(columns, chunk)
        block = rows_all[pl.ds(first, slots)].reshape(chunk, width)
        inner = lax.dot_general(
            cent_ref[...], block, contract_width, preferred_element_type=jnp.float32
        )
        logits = factor * (inner - half_norm)
        peak = jnp.max(logits, axis=0, keepdims=True)
        weight = jnp.exp(logits - peak)
        weights[:, pl.ds(columns, chunk)] = weight
        parts[0, 0:1, pl.ds(columns, chunk)] = peak
        parts[0, 1:2, pl.ds(columns, chunk)] = jnp.sum(weight, axis=0, keepdims=True)
        return carry

    for k in range(shards // slots) if shards // slots <= 4 else ():
        score(k, 0)
    if shards // slots > 4:
        lax.fori_loop(0, shards // slots, score, 0)

    own_peak = parts[0, 0:1, :]

    def joined(part_list):
        highest = part_list[0][0]
        for peak, _ in part_list[1:]:
            highest = jnp.maximum(highest, peak)
        amount = None
        for peak, exp_sum in part_list:
            term = exp_sum * jnp.exp(peak - highest)
            amount = term if amount is None else amount + term
        return highest, amount

    def part(k):
        return parts[k, 0:1, :], parts[k, 1:2, :]

    hop = send(parts.at[0], parts.at[1], p_send.at[0], p_recv.at[0], (g, core_peer))

    def square(k, carry):
        wide = rows_all[k].astype(jnp.float32)
        squares[k] = (wide * wide).astype(jnp.bfloat16)
        return carry

    lax.fori_loop(0, shards, square, 0)
    hop.wait()
    peak, amount = joined([part(0), part(1)])
    parts[2, 0:1, :] = peak
    parts[2, 1:2, :] = amount
    hop = send(parts.at[2], parts.at[3], p_send.at[1], p_recv.at[1], (g, y_peer))
    hop.wait()
    peak, amount = joined([part(2), part(3)])
    parts[4, 0:1, :] = peak
    parts[4, 1:2, :] = amount
    hops = [
        send(parts.at[4], parts.at[4 + s], p_send.at[1 + s], p_recv.at[1 + s], (g, along(s)))
        for s in range(1, line)
    ]
    for hop in hops:
        hop.wait()
    peak, amount = joined([part(4 + s) for s in range(line)])
    lse = peak + jnp.log(amount)
    valid = lax.broadcasted_iota(jnp.int32, (1, total), 1) < length_ref[0]
    scale = jnp.where(valid, jnp.exp(own_peak - lse), 0.0)
    resp = (weights[...] * scale).astype(jnp.bfloat16)

    ones = jnp.ones((8, total), jnp.bfloat16)
    masses[g] = lax.dot_general(ones, resp, contract_width, preferred_element_type=jnp.float32)
    s_copies = {}
    for s in range(1, groups):
        sent.append(
            send(masses.at[g], masses.at[g], m_send.at[s], m_recv.at[s], (across(s), i))
        )
    m_copies = sent[len(sent) - (groups - 1):]
    pieces = 2 * (width // column_step)
    for k in range(pieces):
        left = (k // 2) * column_step
        source = rows_all if k % 2 == 0 else squares
        block = source[:, :, left:left + column_step].reshape(total, column_step)
        sums = lax.dot_general(resp, block, contract_rows, preferred_element_type=jnp.float32)
        stats[g, k] = sums.astype(jnp.bfloat16)
        for s in range(1, groups):
            s_copies[k, s] = send(
                stats.at[g, k], stats.at[g, k], s_send.at[k, s], s_recv.at[k, s], (across(s), i)
            )

    own_lik = jnp.where(valid, lse, 0.0)
    pick = own_lik[:, 0:row_count]
    for j in range(1, shards):
        pick = jnp.where(i == j, own_lik[:, j * row_count:(j + 1) * row_count], pick)
    lik_out[...] = pick

    for copy in m_copies:
        copy.wait_recv()
    mass = masses[0, 0:1, :]
    for r in range(1, groups):
        mass = mass + masses[r, 0:1, :]
    inverse = 1.0 / (mass + prior_weight)
    inverse = jnp.transpose(jnp.broadcast_to(inverse, (cents, cents)))[:, 0:1]
    for k in range(pieces):
        for s in range(1, groups):
            s_copies[k, s].wait_recv()
        left = (k // 2) * column_step
        sums = stats[0, k].astype(jnp.float32)
        for r in range(1, groups):
            sums = sums + stats[r, k].astype(jnp.float32)
        if k % 2 == 0:
            sums = sums + prior_weight * cent_ref[:, left:left + column_step].astype(jnp.float32)
            cent_out[:, left:left + column_step] = (sums * inverse).astype(jnp.bfloat16)
        else:
            mom_out[:, left:left + column_step] = ((sums + prior_weight) * inverse).astype(
                jnp.bfloat16
            )
    for copy in sent + list(s_copies.values()):
        copy.wait_send()


def solution(mesh):
    groups = mesh.shape["rows"]
    shards = mesh.shape["cent"]
    line = shards // 4

    def step(embeddings, centroids, group_length):
        row_count, width = embeddings.shape
        cents = centroids.shape[0]
        total = row_count * shards
        column_step = 256 if width % 256 == 0 else width
        pieces = 2 * (width // column_step)
        vmem = pl.BlockSpec(memory_space=pltpu.VMEM)
        dma = pltpu.SemaphoreType.DMA
        new_centroids, new_moments, loglik = pl.pallas_call(
            functools.partial(kernel, groups, shards, column_step),
            out_shape=(
                jax.ShapeDtypeStruct((cents, width), jnp.bfloat16),
                jax.ShapeDtypeStruct((cents, width), jnp.bfloat16),
                jax.ShapeDtypeStruct((1, row_count), jnp.float32),
            ),
            in_specs=[pl.BlockSpec(memory_space=pltpu.SMEM), vmem, vmem],
            out_specs=(vmem, vmem, vmem),
            scratch_shapes=[
                pltpu.VMEM((shards, row_count, width), jnp.bfloat16),
                pltpu.VMEM((shards, row_count, width), jnp.bfloat16),
                pltpu.VMEM((cents, total), jnp.float32),
                pltpu.VMEM((4 + line, 2, total), jnp.float32),
                pltpu.VMEM((groups, pieces, cents, column_step), jnp.bfloat16),
                pltpu.VMEM((groups, 8, cents), jnp.float32),
                dma, dma((line,)), dma((line,)), dma((line,)), dma((line,)),
                dma((2 * line,)), dma((2 * line,)),
                dma((1 + line,)), dma((1 + line,)),
                dma((pieces, groups)), dma((pieces, groups)),
                dma((groups,)), dma((groups,)),
            ],
            compiler_params=pltpu.CompilerParams(
                collective_id=0, has_side_effects=True, vmem_limit_bytes=56 * 1024 * 1024
            ),
            name="soft_em",
        )(group_length, embeddings, centroids)
        return new_centroids, new_moments, loglik.reshape(row_count)

    return jax.shard_map(
        step,
        mesh=mesh,
        in_specs=(P(("rows", "cent"), None), P("cent", None), P("rows")),
        out_specs=(P("cent", None), P("cent", None), P(("rows", "cent"))),
        check_vma=False,
    )
```

```python
import functools
import math

import jax
import jax.numpy as jnp
from jax import lax
from jax.experimental import pallas as pl
from jax.experimental.pallas import tpu as pltpu
from jax.sharding import PartitionSpec as P

score_factor = 3.0
prior_weight = 1.0
MESH = pl.DeviceIdType.MESH
contract_width = (((1,), (1,)), ((), ()))
contract_rows = (((1,), (0,)), ((), ()))


def kernel(
    groups, shards, column_step, split,
    length_ref, emb_hbm, cent_hbm,
    cent_out, mom_out, lik_out,
    cent_ref, rows_all, squares, weights, parts, stats, masses,
    own_sem, cent_sem, z_send, z_recv, y_send, y_recv, c_send, c_recv,
    p_send, p_recv, s_send, s_recv, m_send, m_recv,
):
    g = lax.axis_index("rows")
    i = lax.axis_index("cent")
    row_count, width = emb_hbm.shape
    cents = cent_ref.shape[0]
    total = shards * row_count
    piece_rows = row_count // split
    line = shards // 4
    spot = lax.rem(i, 4)
    place = i // 4
    core = lax.rem(i, 2)
    core_peer = i + 1 - 2 * core
    y_spot = lax.rem(spot + 2, 4)
    y_peer = place * 4 + y_spot
    factor = score_factor / math.sqrt(width)

    def across(step):
        return lax.rem(g + step, groups)

    def signal(peer):
        pl.semaphore_signal(barrier, inc=1, device_id=peer, device_id_type=MESH)

    barrier = pltpu.get_barrier_semaphore()
    for peer in [(g, y_peer), (g, core_peer)] + [(across(s), i) for s in range(1, groups)]:
        signal(peer)
    has_right = place < line - 1
    has_left = place > 0
    pl.when(has_right)(lambda: signal((g, i + 4)))
    pl.when(has_left)(lambda: signal((g, i - 4)))
    own = [
        pltpu.make_async_copy(
            emb_hbm.at[pl.ds(h * piece_rows, piece_rows)], rows_all.at[i * split + h], own_sem.at[h]
        )
        for h in range(split)
    ]
    for copy in own:
        copy.start()
    cent_copy = pltpu.make_async_copy(cent_hbm, cent_ref, cent_sem)
    cent_copy.start()
    for copy in own:
        copy.wait()
    sides = has_right.astype(jnp.int32) + has_left.astype(jnp.int32)
    pl.semaphore_wait(barrier, 1 + groups + sides)

    def describe(src, dst, send_sem, recv_sem, peer):
        return pltpu.make_async_remote_copy(
            src_ref=src, dst_ref=dst, send_sem=send_sem, recv_sem=recv_sem,
            device_id=peer, device_id_type=MESH,
        )

    def send(*spec):
        copy = describe(*spec)
        copy.start()
        return copy

    def z_copy(unit, way, s, h):
        slot = rows_all.at[unit]
        peer = (g, i + 4 if way == 0 else i - 4)
        return describe(slot, slot, z_send.at[way, s, h], z_recv.at[way, s, h], peer)

    def y_copy(unit, k, h):
        slot = rows_all.at[unit]
        return describe(slot, slot, y_send.at[k, h], y_recv.at[k, h], (g, y_peer))

    def c_copy(unit, k, h):
        slot = rows_all.at[unit]
        return describe(slot, slot, c_send.at[k, h], c_recv.at[k, h], (g, core_peer))

    def square(unit):
        wide = rows_all[unit].astype(jnp.float32)
        squares[unit] = (wide * wide).astype(jnp.bfloat16)

    steps = 2 * line - 1
    order = [(way, s) for s in range(1, line) for way in range(2)]

    def present(way, s):
        return place >= s if way == 0 else place + s < line

    def unit_of(way, s, where, h):
        source = place - s if way == 0 else place + s
        return (source * 4 + where) * split + h

    for h in range(split):
        unit = i * split + h
        pl.when(has_right)(lambda: z_copy(unit, 0, 1, h).start())
        pl.when(has_left)(lambda: z_copy(unit, 1, 1, h).start())
        y_copy(unit, 0, h).start()
        c_copy(unit, 0, h).start()
    for h in range(split):
        square(i * split + h)
    for k, (way, s) in enumerate(order, 1):
        for h in range(split):
            def relay():
                unit = unit_of(way, s, spot, h)
                z_copy(unit, way, s, h).wait_recv()
                onward = has_right if way == 0 else has_left
                if s + 1 < line:
                    pl.when(onward)(lambda: z_copy(unit, way, s + 1, h).start())
                y_copy(unit, k, h).start()
                c_copy(unit, k, h).start()
                square(unit)

            pl.when(present(way, s))(relay)
    for h in range(split):
        unit = unit_of(0, 0, y_spot, h)
        y_copy(unit, 0, h).wait_recv()
        c_copy(unit, steps, h).start()
        square(unit)
    for k, (way, s) in enumerate(order, 1):
        for h in range(split):
            def pass_on():
                unit = unit_of(way, s, y_spot, h)
                y_copy(unit, k, h).wait_recv()
                c_copy(unit, steps + k, h).start()
                square(unit)

            pl.when(present(way, s))(pass_on)
    other = spot + 1 - 2 * core
    for j, where in enumerate((other, lax.rem(other + 2, 4))):
        for h in range(split):
            unit = unit_of(0, 0, where, h)
            c_copy(unit, j * steps, h).wait_recv()
            square(unit)
        for k, (way, s) in enumerate(order, 1):
            for h in range(split):
                def take():
                    unit = unit_of(way, s, where, h)
                    c_copy(unit, j * steps + k, h).wait_recv()
                    square(unit)

                pl.when(present(way, s))(take)
    sent = []
    cent_copy.wait()
    cent_wide = cent_ref[...].astype(jnp.float32)
    half_norm = 0.5 * jnp.sum(cent_wide * cent_wide, axis=1, keepdims=True)

    slots = split * max(1, min(shards, 512 // row_count))
    chunk = slots * piece_rows
    chunks = shards * split // slots

    def score(k, carry):
        first = k * slots
        columns = k * chunk
        if not isinstance(k, int):
            columns = pl.multiple_of(columns, chunk)
        block = rows_all[pl.ds(first, slots)].reshape(chunk, width)
        inner = lax.dot_general(
            cent_ref[...], block, contract_width, preferred_element_type=jnp.float32
        )
        logits = factor * (inner - half_norm)
        peak = jnp.max(logits, axis=0, keepdims=True)
        weight = jnp.exp(logits - peak)
        weights[:, pl.ds(columns, chunk)] = weight
        parts[0, 0:1, pl.ds(columns, chunk)] = peak
        parts[0, 1:2, pl.ds(columns, chunk)] = jnp.sum(weight, axis=0, keepdims=True)
        return carry

    for k in range(chunks) if chunks <= 4 else ():
        score(k, 0)
    if chunks > 4:
        lax.fori_loop(0, chunks, score, 0)

    own_peak = parts[0, 0:1, :]

    def joined(part_list):
        highest = part_list[0][0]
        for peak, _ in part_list[1:]:
            highest = jnp.maximum(highest, peak)
        amount = None
        for peak, exp_sum in part_list:
            term = exp_sum * jnp.exp(peak - highest)
            amount = term if amount is None else amount + term
        return highest, amount

    def part(k):
        return parts[k, 0:1, :], parts[k, 1:2, :]

    hop = send(parts.at[0], parts.at[1], p_send.at[0], p_recv.at[0], (g, core_peer))

    hop.wait()
    peak, amount = joined([part(0), part(1)])
    parts[2, 0:1, :] = peak
    parts[2, 1:2, :] = amount
    hops = []
    for k in range(2 * line - 1, 0, -1):
        peer = lax.rem(place + k // 2, line) * 4 + lax.rem(spot + 2 * (k % 2), 4)
        hops.append(send(parts.at[2], parts.at[2 + k], p_send.at[k], p_recv.at[k], (g, peer)))
    for hop in hops:
        hop.wait_recv()
    sent += hops
    peak, amount = joined([part(2 + k) for k in range(2 * line)])
    lse = peak + jnp.log(amount)
    valid = lax.broadcasted_iota(jnp.int32, (1, total), 1) < length_ref[0]
    scale = jnp.where(valid, jnp.exp(own_peak - lse), 0.0)
    resp = (weights[...] * scale).astype(jnp.bfloat16)

    ones = jnp.ones((8, total), jnp.bfloat16)
    masses[g] = lax.dot_general(ones, resp, contract_width, preferred_element_type=jnp.float32)
    s_copies = {}
    for s in range(1, groups):
        sent.append(
            send(masses.at[g], masses.at[g], m_send.at[s], m_recv.at[s], (across(s), i))
        )
    m_copies = sent[len(sent) - (groups - 1):]
    pieces = 2 * (width // column_step)
    for k in range(pieces):
        left = (k // 2) * column_step
        source = rows_all if k % 2 == 0 else squares
        block = source[:, :, left:left + column_step].reshape(total, column_step)
        sums = lax.dot_general(resp, block, contract_rows, preferred_element_type=jnp.float32)
        stats[g, k] = sums.astype(jnp.bfloat16)
        for s in range(1, groups):
            s_copies[k, s] = send(
                stats.at[g, k], stats.at[g, k], s_send.at[k, s], s_recv.at[k, s], (across(s), i)
            )

    own_lik = jnp.where(valid, lse, 0.0)
    pick = own_lik[:, 0:row_count]
    for j in range(1, shards):
        pick = jnp.where(i == j, own_lik[:, j * row_count:(j + 1) * row_count], pick)
    lik_out[...] = pick

    for copy in m_copies:
        copy.wait_recv()
    mass = masses[0, 0:1, :]
    for r in range(1, groups):
        mass = mass + masses[r, 0:1, :]
    inverse = 1.0 / (mass + prior_weight)
    inverse = jnp.transpose(jnp.broadcast_to(inverse, (cents, cents)))[:, 0:1]
    for k in range(pieces):
        for s in range(1, groups):
            s_copies[k, s].wait_recv()
        left = (k // 2) * column_step
        sums = stats[0, k].astype(jnp.float32)
        for r in range(1, groups):
            sums = sums + stats[r, k].astype(jnp.float32)
        if k % 2 == 0:
            sums = sums + prior_weight * cent_ref[:, left:left + column_step].astype(jnp.float32)
            cent_out[:, left:left + column_step] = (sums * inverse).astype(jnp.bfloat16)
        else:
            mom_out[:, left:left + column_step] = ((sums + prior_weight) * inverse).astype(
                jnp.bfloat16
            )
    for h in range(split):
        unit = i * split + h
        pl.when(has_right)(lambda: z_copy(unit, 0, 1, h).wait_send())
        pl.when(has_left)(lambda: z_copy(unit, 1, 1, h).wait_send())
        y_copy(unit, 0, h).wait_send()
        c_copy(unit, 0, h).wait_send()
        c_copy(unit_of(0, 0, y_spot, h), steps, h).wait_send()
    for k, (way, s) in enumerate(order, 1):
        for h in range(split):
            def finish():
                unit = unit_of(way, s, spot, h)
                onward = has_right if way == 0 else has_left
                if s + 1 < line:
                    pl.when(onward)(lambda: z_copy(unit, way, s + 1, h).wait_send())
                y_copy(unit, k, h).wait_send()
                c_copy(unit, k, h).wait_send()
                c_copy(unit_of(way, s, y_spot, h), steps + k, h).wait_send()

            pl.when(present(way, s))(finish)
    for copy in sent + list(s_copies.values()):
        copy.wait_send()


def solution(mesh):
    groups = mesh.shape["rows"]
    shards = mesh.shape["cent"]
    line = shards // 4

    def step(embeddings, centroids, group_length):
        row_count, width = embeddings.shape
        cents = centroids.shape[0]
        total = row_count * shards
        column_step = 256 if width % 256 == 0 else width
        pieces = 2 * (width // column_step)
        split = 2 if row_count % 32 == 0 else 1
        vmem = pl.BlockSpec(memory_space=pltpu.VMEM)
        hbm = pl.BlockSpec(memory_space=pltpu.HBM)
        held = 4 * total * width + 4 * cents * total + 2 * (groups * 2 + 1) * cents * width
        steps = 2 * line - 1
        dma = pltpu.SemaphoreType.DMA
        new_centroids, new_moments, loglik = pl.pallas_call(
            functools.partial(kernel, groups, shards, column_step, split),
            out_shape=(
                jax.ShapeDtypeStruct((cents, width), jnp.bfloat16),
                jax.ShapeDtypeStruct((cents, width), jnp.bfloat16),
                jax.ShapeDtypeStruct((1, row_count), jnp.float32),
            ),
            in_specs=[pl.BlockSpec(memory_space=pltpu.SMEM), hbm, hbm],
            out_specs=(vmem, vmem, vmem),
            scratch_shapes=[
                pltpu.VMEM((cents, width), jnp.bfloat16),
                pltpu.VMEM((shards * split, row_count // split, width), jnp.bfloat16),
                pltpu.VMEM((shards * split, row_count // split, width), jnp.bfloat16),
                pltpu.VMEM((cents, total), jnp.float32),
                pltpu.VMEM((2 + 2 * line, 2, total), jnp.float32),
                pltpu.VMEM((groups, pieces, cents, column_step), jnp.bfloat16),
                pltpu.VMEM((groups, 8, cents), jnp.float32),
                dma((split,)), dma, dma((2, line, split)), dma((2, line, split)),
                dma((steps, split)), dma((steps, split)),
                dma((2 * steps, split)), dma((2 * steps, split)),
                dma((2 * line,)), dma((2 * line,)),
                dma((pieces, groups)), dma((pieces, groups)),
                dma((groups,)), dma((groups,)),
            ],
            compiler_params=pltpu.CompilerParams(
                collective_id=0, has_side_effects=True, vmem_limit_bytes=2 * held + 4 * 1024 * 1024
            ),
            name="soft_em",
        )(group_length, embeddings, centroids)
        return new_centroids, new_moments, loglik.reshape(row_count)

    return jax.shard_map(
        step,
        mesh=mesh,
        in_specs=(P(("rows", "cent"), None), P("cent", None), P("rows")),
        out_specs=(P("cent", None), P("cent", None), P(("rows", "cent"))),
        check_vma=False,
    )
```

```python
import functools
import math

import jax
import jax.numpy as jnp
from jax import lax
from jax.experimental import pallas as pl
from jax.experimental.pallas import tpu as pltpu
from jax.sharding import PartitionSpec as P

score_factor = 3.0
prior_weight = 1.0
MESH = pl.DeviceIdType.MESH
contract_width = (((1,), (1,)), ((), ()))
contract_rows = (((1,), (0,)), ((), ()))


def kernel(
    groups, shards, column_step, split,
    length_ref, emb_hbm, cent_hbm,
    cent_out, mom_out, lik_out,
    cent_ref, rows_all, squares, weights, parts, stats, masses,
    own_sem, cent_sem, z_send, z_recv, y_send, y_recv, c_send, c_recv,
    p_send, p_recv, s_send, s_recv, m_send, m_recv,
):
    g = lax.axis_index("rows")
    i = lax.axis_index("cent")
    row_count, width = emb_hbm.shape
    cents = cent_ref.shape[0]
    total = shards * row_count
    piece_rows = row_count // split
    line = shards // 4
    spot = lax.rem(i, 4)
    place = i // 4
    core = lax.rem(i, 2)
    core_peer = i + 1 - 2 * core
    y_spot = lax.rem(spot + 2, 4)
    y_peer = place * 4 + y_spot
    factor = score_factor / math.sqrt(width)

    def across(step):
        return lax.rem(g + step, groups)

    def signal(peer):
        pl.semaphore_signal(barrier, inc=1, device_id=peer, device_id_type=MESH)

    barrier = pltpu.get_barrier_semaphore()
    for peer in [(g, y_peer), (g, core_peer)] + [(across(s), i) for s in range(1, groups)]:
        signal(peer)
    has_right = place < line - 1
    has_left = place > 0
    pl.when(has_right)(lambda: signal((g, i + 4)))
    pl.when(has_left)(lambda: signal((g, i - 4)))
    own = [
        pltpu.make_async_copy(
            emb_hbm.at[pl.ds(h * piece_rows, piece_rows)], rows_all.at[i * split + h], own_sem.at[h]
        )
        for h in range(split)
    ]
    for copy in own:
        copy.start()
    cent_copy = pltpu.make_async_copy(cent_hbm, cent_ref, cent_sem)
    cent_copy.start()
    for copy in own:
        copy.wait()
    sides = has_right.astype(jnp.int32) + has_left.astype(jnp.int32)
    pl.semaphore_wait(barrier, 1 + groups + sides)

    def describe(src, dst, send_sem, recv_sem, peer):
        return pltpu.make_async_remote_copy(
            src_ref=src, dst_ref=dst, send_sem=send_sem, recv_sem=recv_sem,
            device_id=peer, device_id_type=MESH,
        )

    def send(*spec):
        copy = describe(*spec)
        copy.start()
        return copy

    def z_copy(unit, way, s, h):
        slot = rows_all.at[unit]
        peer = (g, i + 4 if way == 0 else i - 4)
        return describe(slot, slot, z_send.at[way, s, h], z_recv.at[way, s, h], peer)

    def y_copy(unit, k, h):
        slot = rows_all.at[unit]
        return describe(slot, slot, y_send.at[k, h], y_recv.at[k, h], (g, y_peer))

    def c_copy(unit, k, h):
        slot = rows_all.at[unit]
        return describe(slot, slot, c_send.at[k, h], c_recv.at[k, h], (g, core_peer))

    def square(unit):
        wide = rows_all[unit].astype(jnp.float32)
        squares[unit] = (wide * wide).astype(jnp.bfloat16)

    steps = 2 * line - 1
    order = [(way, s) for s in range(1, line) for way in range(2)]

    def present(way, s):
        return place >= s if way == 0 else place + s < line

    def unit_of(way, s, where, h):
        source = place - s if way == 0 else place + s
        return (source * 4 + where) * split + h

    for h in range(split):
        unit = i * split + h
        pl.when(has_right)(lambda: z_copy(unit, 0, 1, h).start())
        pl.when(has_left)(lambda: z_copy(unit, 1, 1, h).start())
        y_copy(unit, 0, h).start()
        c_copy(unit, 0, h).start()
    for h in range(split):
        square(i * split + h)
    for k, (way, s) in enumerate(order, 1):
        for h in range(split):
            def relay():
                unit = unit_of(way, s, spot, h)
                z_copy(unit, way, s, h).wait_recv()
                onward = has_right if way == 0 else has_left
                if s + 1 < line:
                    pl.when(onward)(lambda: z_copy(unit, way, s + 1, h).start())
                y_copy(unit, k, h).start()
                c_copy(unit, k, h).start()
                square(unit)

            pl.when(present(way, s))(relay)
    for h in range(split):
        unit = unit_of(0, 0, y_spot, h)
        y_copy(unit, 0, h).wait_recv()
        c_copy(unit, steps, h).start()
        square(unit)
    for k, (way, s) in enumerate(order, 1):
        for h in range(split):
            def pass_on():
                unit = unit_of(way, s, y_spot, h)
                y_copy(unit, k, h).wait_recv()
                c_copy(unit, steps + k, h).start()
                square(unit)

            pl.when(present(way, s))(pass_on)
    other = spot + 1 - 2 * core
    for j, where in enumerate((other, lax.rem(other + 2, 4))):
        for h in range(split):
            unit = unit_of(0, 0, where, h)
            c_copy(unit, j * steps, h).wait_recv()
            square(unit)
        for k, (way, s) in enumerate(order, 1):
            for h in range(split):
                def take():
                    unit = unit_of(way, s, where, h)
                    c_copy(unit, j * steps + k, h).wait_recv()
                    square(unit)

                pl.when(present(way, s))(take)
    sent = []
    cent_copy.wait()
    cent_wide = cent_ref[...].astype(jnp.float32)
    half_norm = 0.5 * jnp.sum(cent_wide * cent_wide, axis=1, keepdims=True)

    slots = split * max(1, min(shards, 512 // row_count))
    chunk = slots * piece_rows
    chunks = shards * split // slots

    def score(k, carry):
        first = k * slots
        columns = k * chunk
        if not isinstance(k, int):
            columns = pl.multiple_of(columns, chunk)
        block = rows_all[pl.ds(first, slots)].reshape(chunk, width)
        inner = lax.dot_general(
            cent_ref[...], block, contract_width, preferred_element_type=jnp.float32
        )
        logits = factor * (inner - half_norm)
        peak = jnp.max(logits, axis=0, keepdims=True)
        weight = jnp.exp(logits - peak)
        weights[:, pl.ds(columns, chunk)] = weight
        parts[0, 0:1, pl.ds(columns, chunk)] = peak
        parts[0, 1:2, pl.ds(columns, chunk)] = jnp.sum(weight, axis=0, keepdims=True)
        return carry

    for k in range(chunks) if chunks <= 4 else ():
        score(k, 0)
    if chunks > 4:
        lax.fori_loop(0, chunks, score, 0)

    own_peak = parts[0, 0:1, :]

    def joined(part_list):
        highest = part_list[0][0]
        for peak, _ in part_list[1:]:
            highest = jnp.maximum(highest, peak)
        amount = None
        for peak, exp_sum in part_list:
            term = exp_sum * jnp.exp(peak - highest)
            amount = term if amount is None else amount + term
        return highest, amount

    def part(k):
        return parts[k, 0:1, :], parts[k, 1:2, :]

    hop = send(parts.at[0], parts.at[1], p_send.at[0], p_recv.at[0], (g, core_peer))

    hop.wait()
    peak, amount = joined([part(0), part(1)])
    parts[2, 0:1, :] = peak
    parts[2, 1:2, :] = amount
    hops = []
    for k in range(2 * line - 1, 0, -1):
        peer = lax.rem(place + k // 2, line) * 4 + lax.rem(spot + 2 * (k % 2), 4)
        hops.append(send(parts.at[2], parts.at[2 + k], p_send.at[k], p_recv.at[k], (g, peer)))
    for hop in hops:
        hop.wait_recv()
    sent += hops
    peak, amount = joined([part(2 + k) for k in range(2 * line)])
    lse = peak + jnp.log(amount)
    valid = lax.broadcasted_iota(jnp.int32, (1, total), 1) < length_ref[0]
    scale = jnp.where(valid, jnp.exp(own_peak - lse), 0.0)
    resp = (weights[...] * scale).astype(jnp.bfloat16)

    ones = jnp.ones((8, total), jnp.bfloat16)
    masses[g] = lax.dot_general(ones, resp, contract_width, preferred_element_type=jnp.float32)
    s_copies = {}
    for s in range(1, groups):
        sent.append(
            send(masses.at[g], masses.at[g], m_send.at[s], m_recv.at[s], (across(s), i))
        )
    m_copies = sent[len(sent) - (groups - 1):]
    pieces = 2 * (width // column_step)
    for k in range(pieces):
        left = (k // 2) * column_step
        source = rows_all if k % 2 == 0 else squares
        block = source[:, :, left:left + column_step].reshape(total, column_step)
        sums = lax.dot_general(resp, block, contract_rows, preferred_element_type=jnp.float32)
        stats[g, k] = sums.astype(jnp.bfloat16)
        for s in range(1, groups):
            s_copies[k, s] = send(
                stats.at[g, k], stats.at[g, k], s_send.at[k, s], s_recv.at[k, s], (across(s), i)
            )

    own_lik = jnp.where(valid, lse, 0.0)
    pick = own_lik[:, 0:row_count]
    for j in range(1, shards):
        pick = jnp.where(i == j, own_lik[:, j * row_count:(j + 1) * row_count], pick)
    lik_out[...] = pick

    for copy in m_copies:
        copy.wait_recv()
    mass = masses[0, 0:1, :]
    for r in range(1, groups):
        mass = mass + masses[r, 0:1, :]
    inverse = 1.0 / (mass + prior_weight)
    inverse = jnp.transpose(jnp.broadcast_to(inverse, (cents, cents)))[:, 0:1]
    for k in range(pieces):
        for s in range(1, groups):
            s_copies[k, s].wait_recv()
        left = (k // 2) * column_step
        sums = stats[0, k].astype(jnp.float32)
        for r in range(1, groups):
            sums = sums + stats[r, k].astype(jnp.float32)
        if k % 2 == 0:
            sums = sums + prior_weight * cent_ref[:, left:left + column_step].astype(jnp.float32)
            cent_out[:, left:left + column_step] = (sums * inverse).astype(jnp.bfloat16)
        else:
            mom_out[:, left:left + column_step] = ((sums + prior_weight) * inverse).astype(
                jnp.bfloat16
            )
    for h in range(split):
        unit = i * split + h
        pl.when(has_right)(lambda: z_copy(unit, 0, 1, h).wait_send())
        pl.when(has_left)(lambda: z_copy(unit, 1, 1, h).wait_send())
        y_copy(unit, 0, h).wait_send()
        c_copy(unit, 0, h).wait_send()
        c_copy(unit_of(0, 0, y_spot, h), steps, h).wait_send()
    for k, (way, s) in enumerate(order, 1):
        for h in range(split):
            def finish():
                unit = unit_of(way, s, spot, h)
                onward = has_right if way == 0 else has_left
                if s + 1 < line:
                    pl.when(onward)(lambda: z_copy(unit, way, s + 1, h).wait_send())
                y_copy(unit, k, h).wait_send()
                c_copy(unit, k, h).wait_send()
                c_copy(unit_of(way, s, y_spot, h), steps + k, h).wait_send()

            pl.when(present(way, s))(finish)
    for copy in sent + list(s_copies.values()):
        copy.wait_send()


def solution(mesh):
    groups = mesh.shape["rows"]
    shards = mesh.shape["cent"]
    line = shards // 4

    def step(embeddings, centroids, group_length):
        row_count, width = embeddings.shape
        cents = centroids.shape[0]
        total = row_count * shards
        column_step = 256 if width % 256 == 0 else width
        pieces = 2 * (width // column_step)
        split = 2 if row_count % 32 == 0 else 1
        vmem = pl.BlockSpec(memory_space=pltpu.VMEM)
        hbm = pl.BlockSpec(memory_space=pltpu.HBM)
        held = 4 * total * width + 4 * cents * total + 2 * (groups * 2 + 1) * cents * width
        steps = 2 * line - 1
        dma = pltpu.SemaphoreType.DMA
        new_centroids, new_moments, loglik = pl.pallas_call(
            functools.partial(kernel, groups, shards, column_step, split),
            out_shape=(
                jax.ShapeDtypeStruct((cents, width), jnp.bfloat16),
                jax.ShapeDtypeStruct((cents, width), jnp.bfloat16),
                jax.ShapeDtypeStruct((1, row_count), jnp.float32),
            ),
            in_specs=[pl.BlockSpec(memory_space=pltpu.SMEM), hbm, hbm],
            out_specs=(vmem, vmem, vmem),
            scratch_shapes=[
                pltpu.VMEM((cents, width), jnp.bfloat16),
                pltpu.VMEM((shards * split, row_count // split, width), jnp.bfloat16),
                pltpu.VMEM((shards * split, row_count // split, width), jnp.bfloat16),
                pltpu.VMEM((cents, total), jnp.float32),
                pltpu.VMEM((2 + 2 * line, 2, total), jnp.float32),
                pltpu.VMEM((groups, pieces, cents, column_step), jnp.bfloat16),
                pltpu.VMEM((groups, 8, cents), jnp.float32),
                dma((split,)), dma, dma((2, line, split)), dma((2, line, split)),
                dma((steps, split)), dma((steps, split)),
                dma((2 * steps, split)), dma((2 * steps, split)),
                dma((2 * line,)), dma((2 * line,)),
                dma((pieces, groups)), dma((pieces, groups)),
                dma((groups,)), dma((groups,)),
            ],
            compiler_params=pltpu.CompilerParams(
                collective_id=0, has_side_effects=True, vmem_limit_bytes=2 * held + 4 * 1024 * 1024
            ),
            name="soft_em",
        )(group_length, pltpu.with_memory_space_constraint(embeddings, pltpu.HBM), pltpu.with_memory_space_constraint(centroids, pltpu.HBM))
        return new_centroids, new_moments, loglik.reshape(row_count)

    return jax.shard_map(
        step,
        mesh=mesh,
        in_specs=(P(("rows", "cent"), None), P("cent", None), P("rows")),
        out_specs=(P("cent", None), P("cent", None), P(("rows", "cent"))),
        check_vma=False,
    )
```

```python
import functools
import math

import jax
import jax.numpy as jnp
from jax import lax
from jax.experimental import pallas as pl
from jax.experimental.pallas import tpu as pltpu
from jax.sharding import PartitionSpec as P

score_factor = 3.0
prior_weight = 1.0
MESH = pl.DeviceIdType.MESH
contract_width = (((1,), (1,)), ((), ()))
contract_rows = (((1,), (0,)), ((), ()))


def kernel(
    groups, shards, column_step, split,
    length_ref, emb_hbm, cent_hbm,
    cent_out, mom_out, lik_out, inverse_out,
    cent_ref, rows_all, squares, weights, parts, stats, masses,
    own_sem, cent_sem, z_send, z_recv, y_send, y_recv, c_send, c_recv,
    p_send, p_recv, s_send, s_recv, m_send, m_recv,
):
    g = lax.axis_index("rows")
    i = lax.axis_index("cent")
    row_count, width = emb_hbm.shape
    cents = cent_ref.shape[0]
    total = shards * row_count
    piece_rows = row_count // split
    line = shards // 4
    spot = lax.rem(i, 4)
    place = i // 4
    core = lax.rem(i, 2)
    core_peer = i + 1 - 2 * core
    y_spot = lax.rem(spot + 2, 4)
    y_peer = place * 4 + y_spot
    factor = score_factor / math.sqrt(width)

    def across(step):
        return lax.rem(g + step, groups)

    def signal(peer):
        pl.semaphore_signal(barrier, inc=1, device_id=peer, device_id_type=MESH)

    barrier = pltpu.get_barrier_semaphore()
    for peer in [(g, y_peer), (g, core_peer)] + [(across(s), i) for s in range(1, groups)]:
        signal(peer)
    has_right = place < line - 1
    has_left = place > 0
    pl.when(has_right)(lambda: signal((g, i + 4)))
    pl.when(has_left)(lambda: signal((g, i - 4)))
    own = [
        pltpu.make_async_copy(
            emb_hbm.at[pl.ds(h * piece_rows, piece_rows)], rows_all.at[i * split + h], own_sem.at[h]
        )
        for h in range(split)
    ]
    for copy in own:
        copy.start()
    cent_copy = pltpu.make_async_copy(cent_hbm, cent_ref, cent_sem)
    cent_copy.start()
    for copy in own:
        copy.wait()
    sides = has_right.astype(jnp.int32) + has_left.astype(jnp.int32)
    pl.semaphore_wait(barrier, 1 + groups + sides)

    def describe(src, dst, send_sem, recv_sem, peer):
        return pltpu.make_async_remote_copy(
            src_ref=src, dst_ref=dst, send_sem=send_sem, recv_sem=recv_sem,
            device_id=peer, device_id_type=MESH,
        )

    def send(*spec):
        copy = describe(*spec)
        copy.start()
        return copy

    def z_copy(unit, way, s, h):
        slot = rows_all.at[unit]
        peer = (g, i + 4 if way == 0 else i - 4)
        return describe(slot, slot, z_send.at[way, s, h], z_recv.at[way, s, h], peer)

    def y_copy(unit, k, h):
        slot = rows_all.at[unit]
        return describe(slot, slot, y_send.at[k, h], y_recv.at[k, h], (g, y_peer))

    def c_copy(unit, k, h):
        slot = rows_all.at[unit]
        return describe(slot, slot, c_send.at[k, h], c_recv.at[k, h], (g, core_peer))

    def square(unit):
        wide = rows_all[unit].astype(jnp.float32)
        squares[unit] = (wide * wide).astype(jnp.bfloat16)

    steps = 2 * line - 1
    order = [(way, s) for s in range(1, line) for way in range(2)]

    def present(way, s):
        return place >= s if way == 0 else place + s < line

    def unit_of(way, s, where, h):
        source = place - s if way == 0 else place + s
        return (source * 4 + where) * split + h

    for h in range(split):
        unit = i * split + h
        pl.when(has_right)(lambda: z_copy(unit, 0, 1, h).start())
        pl.when(has_left)(lambda: z_copy(unit, 1, 1, h).start())
        y_copy(unit, 0, h).start()
        c_copy(unit, 0, h).start()
    for h in range(split):
        square(i * split + h)
    for k, (way, s) in enumerate(order, 1):
        for h in range(split):
            def relay():
                unit = unit_of(way, s, spot, h)
                z_copy(unit, way, s, h).wait_recv()
                onward = has_right if way == 0 else has_left
                if s + 1 < line:
                    pl.when(onward)(lambda: z_copy(unit, way, s + 1, h).start())
                y_copy(unit, k, h).start()
                c_copy(unit, k, h).start()
                square(unit)

            pl.when(present(way, s))(relay)
    for h in range(split):
        unit = unit_of(0, 0, y_spot, h)
        y_copy(unit, 0, h).wait_recv()
        c_copy(unit, steps, h).start()
        square(unit)
    for k, (way, s) in enumerate(order, 1):
        for h in range(split):
            def pass_on():
                unit = unit_of(way, s, y_spot, h)
                y_copy(unit, k, h).wait_recv()
                c_copy(unit, steps + k, h).start()
                square(unit)

            pl.when(present(way, s))(pass_on)
    other = spot + 1 - 2 * core
    for j, where in enumerate((other, lax.rem(other + 2, 4))):
        for h in range(split):
            unit = unit_of(0, 0, where, h)
            c_copy(unit, j * steps, h).wait_recv()
            square(unit)
        for k, (way, s) in enumerate(order, 1):
            for h in range(split):
                def take():
                    unit = unit_of(way, s, where, h)
                    c_copy(unit, j * steps + k, h).wait_recv()
                    square(unit)

                pl.when(present(way, s))(take)
    sent = []
    cent_copy.wait()
    cent_wide = cent_ref[...].astype(jnp.float32)
    half_norm = 0.5 * jnp.sum(cent_wide * cent_wide, axis=1, keepdims=True)

    slots = split * max(1, min(shards, 512 // row_count))
    chunk = slots * piece_rows
    chunks = shards * split // slots

    def score(k, carry):
        first = k * slots
        columns = k * chunk
        if not isinstance(k, int):
            columns = pl.multiple_of(columns, chunk)
        block = rows_all[pl.ds(first, slots)].reshape(chunk, width)
        inner = lax.dot_general(
            cent_ref[...], block, contract_width, preferred_element_type=jnp.float32
        )
        logits = factor * (inner - half_norm)
        peak = jnp.max(logits, axis=0, keepdims=True)
        weight = jnp.exp(logits - peak)
        weights[:, pl.ds(columns, chunk)] = weight
        parts[0, 0:1, pl.ds(columns, chunk)] = peak
        parts[0, 1:2, pl.ds(columns, chunk)] = jnp.sum(weight, axis=0, keepdims=True)
        return carry

    for k in range(chunks) if chunks <= 4 else ():
        score(k, 0)
    if chunks > 4:
        lax.fori_loop(0, chunks, score, 0)

    own_peak = parts[0, 0:1, :]

    def joined(part_list):
        highest = part_list[0][0]
        for peak, _ in part_list[1:]:
            highest = jnp.maximum(highest, peak)
        amount = None
        for peak, exp_sum in part_list:
            term = exp_sum * jnp.exp(peak - highest)
            amount = term if amount is None else amount + term
        return highest, amount

    def part(k):
        return parts[k, 0:1, :], parts[k, 1:2, :]

    hop = send(parts.at[0], parts.at[1], p_send.at[0], p_recv.at[0], (g, core_peer))

    hop.wait()
    peak, amount = joined([part(0), part(1)])
    parts[2, 0:1, :] = peak
    parts[2, 1:2, :] = amount
    hops = []
    for k in range(2 * line - 1, 0, -1):
        peer = lax.rem(place + k // 2, line) * 4 + lax.rem(spot + 2 * (k % 2), 4)
        hops.append(send(parts.at[2], parts.at[2 + k], p_send.at[k], p_recv.at[k], (g, peer)))
    for hop in hops:
        hop.wait_recv()
    sent += hops
    peak, amount = joined([part(2 + k) for k in range(2 * line)])
    lse = peak + jnp.log(amount)
    valid = lax.broadcasted_iota(jnp.int32, (1, total), 1) < length_ref[0]
    scale = jnp.where(valid, jnp.exp(own_peak - lse), 0.0)
    resp = (weights[...] * scale).astype(jnp.bfloat16)

    ones = jnp.ones((8, total), jnp.bfloat16)
    masses[g] = lax.dot_general(ones, resp, contract_width, preferred_element_type=jnp.float32)
    s_copies = {}
    for s in range(1, groups):
        sent.append(
            send(masses.at[g], masses.at[g], m_send.at[s], m_recv.at[s], (across(s), i))
        )
    m_copies = sent[len(sent) - (groups - 1):]
    pieces = 2 * (width // column_step)
    for k in range(pieces):
        left = (k // 2) * column_step
        source = rows_all if k % 2 == 0 else squares
        block = source[:, :, left:left + column_step].reshape(total, column_step)
        sums = lax.dot_general(resp, block, contract_rows, preferred_element_type=jnp.float32)
        stats[g, k] = sums.astype(jnp.bfloat16)
        for s in range(1, groups):
            s_copies[k, s] = send(
                stats.at[g, k], stats.at[g, k], s_send.at[k, s], s_recv.at[k, s], (across(s), i)
            )

    own_lik = jnp.where(valid, lse, 0.0)
    pick = own_lik[:, 0:row_count]
    for j in range(1, shards):
        pick = jnp.where(i == j, own_lik[:, j * row_count:(j + 1) * row_count], pick)
    lik_out[...] = pick

    for copy in m_copies:
        copy.wait_recv()
    mass = masses[0, 0:1, :]
    for r in range(1, groups):
        mass = mass + masses[r, 0:1, :]
    inverse = 1.0 / (mass + prior_weight)
    inverse_out[...] = jnp.transpose(jnp.broadcast_to(inverse, (cents, cents)))
    for k in range(pieces):
        for s in range(1, groups):
            s_copies[k, s].wait_recv()
        left = (k // 2) * column_step
        sums = stats[0, k].astype(jnp.float32)
        for r in range(1, groups):
            sums = sums + stats[r, k].astype(jnp.float32)
        if k % 2 == 0:
            sums = sums + prior_weight * cent_ref[:, left:left + column_step].astype(jnp.float32)
            cent_out[:, left:left + column_step] = sums
        else:
            mom_out[:, left:left + column_step] = sums + prior_weight
    for h in range(split):
        unit = i * split + h
        pl.when(has_right)(lambda: z_copy(unit, 0, 1, h).wait_send())
        pl.when(has_left)(lambda: z_copy(unit, 1, 1, h).wait_send())
        y_copy(unit, 0, h).wait_send()
        c_copy(unit, 0, h).wait_send()
        c_copy(unit_of(0, 0, y_spot, h), steps, h).wait_send()
    for k, (way, s) in enumerate(order, 1):
        for h in range(split):
            def finish():
                unit = unit_of(way, s, spot, h)
                onward = has_right if way == 0 else has_left
                if s + 1 < line:
                    pl.when(onward)(lambda: z_copy(unit, way, s + 1, h).wait_send())
                y_copy(unit, k, h).wait_send()
                c_copy(unit, k, h).wait_send()
                c_copy(unit_of(way, s, y_spot, h), steps + k, h).wait_send()

            pl.when(present(way, s))(finish)
    for copy in sent + list(s_copies.values()):
        copy.wait_send()


def solution(mesh):
    groups = mesh.shape["rows"]
    shards = mesh.shape["cent"]
    line = shards // 4

    def step(embeddings, centroids, group_length):
        row_count, width = embeddings.shape
        cents = centroids.shape[0]
        total = row_count * shards
        column_step = 256 if width % 256 == 0 else width
        pieces = 2 * (width // column_step)
        split = 2 if row_count % 32 == 0 else 1
        vmem = pl.BlockSpec(memory_space=pltpu.VMEM)
        hbm = pl.BlockSpec(memory_space=pltpu.HBM)
        held = 4 * total * width + 4 * cents * total + 2 * (groups * 2 + 1) * cents * width
        steps = 2 * line - 1
        dma = pltpu.SemaphoreType.DMA
        cent_sums, moment_sums, loglik, inverse = pl.pallas_call(
            functools.partial(kernel, groups, shards, column_step, split),
            out_shape=(
                jax.ShapeDtypeStruct((cents, width), jnp.float32),
                jax.ShapeDtypeStruct((cents, width), jnp.float32),
                jax.ShapeDtypeStruct((1, row_count), jnp.float32),
                jax.ShapeDtypeStruct((cents, cents), jnp.float32),
            ),
            in_specs=[pl.BlockSpec(memory_space=pltpu.SMEM), hbm, hbm],
            out_specs=(vmem, vmem, vmem, vmem),
            scratch_shapes=[
                pltpu.VMEM((cents, width), jnp.bfloat16),
                pltpu.VMEM((shards * split, row_count // split, width), jnp.bfloat16),
                pltpu.VMEM((shards * split, row_count // split, width), jnp.bfloat16),
                pltpu.VMEM((cents, total), jnp.float32),
                pltpu.VMEM((2 + 2 * line, 2, total), jnp.float32),
                pltpu.VMEM((groups, pieces, cents, column_step), jnp.bfloat16),
                pltpu.VMEM((groups, 8, cents), jnp.float32),
                dma((split,)), dma, dma((2, line, split)), dma((2, line, split)),
                dma((steps, split)), dma((steps, split)),
                dma((2 * steps, split)), dma((2 * steps, split)),
                dma((2 * line,)), dma((2 * line,)),
                dma((pieces, groups)), dma((pieces, groups)),
                dma((groups,)), dma((groups,)),
            ],
            compiler_params=pltpu.CompilerParams(
                collective_id=0, has_side_effects=True, vmem_limit_bytes=2 * held + 4 * 1024 * 1024
            ),
            name="soft_em",
        )(group_length, pltpu.with_memory_space_constraint(embeddings, pltpu.HBM), pltpu.with_memory_space_constraint(centroids, pltpu.HBM))
        new_centroids = (cent_sums * inverse[:, 0:1]).astype(jnp.bfloat16)
        new_moments = (moment_sums * inverse[:, 0:1]).astype(jnp.bfloat16)
        return new_centroids, new_moments, loglik.reshape(row_count)

    return jax.shard_map(
        step,
        mesh=mesh,
        in_specs=(P(("rows", "cent"), None), P("cent", None), P("rows")),
        out_specs=(P("cent", None), P("cent", None), P(("rows", "cent"))),
        check_vma=False,
    )
```
